32 devices in a mesh: clip: 4 (over y, x), tm: 4 (over z), space: 2 (over core).
Axes of the slice: x: 2, y: 2, z: 4, core: 2. Of those that a mesh axis runs over, the one named last changes fastest.
Arguments:
- latents: bfloat16 [8, 8, 4, 64, 384], P('clip', 'tm', 'space'), parts along dimension 0, may hold values from -6 to 6
- frame_counts: int32 [8], P('clip'), parts along dimension 0, may hold values from 1 to 8, as said below
- norm_gain: float32 [384], replicated, may hold values from 0.1 to 1.9
- norm_bias: float32 [384], replicated, may hold values from -3 to 3
- conv3_weight: bfloat16 [3, 3, 3, 384, 384], replicated, may hold values from -0.0625 to 0.0625
- conv3_bias: float32 [384], replicated, may hold values from -3 to 3
- conv2_weight: bfloat16 [3, 3, 384, 384], replicated, may hold values from -0.109375 to 0.109375
- conv2_bias: float32 [384], replicated, may hold values from -3 to 3
Outputs:
- decoded: bfloat16 [8, 8, 8, 128, 384], P('clip', 'tm', 'space'), parts along dimension 0
The draws below stay inside these ranges and needn't reach their ends.
There are 4 independent parts, one for each index of `clip`. The reference program is written for one: setup_inputs(seed, part) draws one part's arguments, and reference() takes and returns one part's arrays. A program takes and returns all parts, laid end to end along the dimension named above; an argument that names none is the same for every part. Nothing has to cross between parts.
Inputs may be any that keep to these rules, and one draw needn't show every extreme that they name: `frame_counts`: each clip has between 1 and 8 real frames; in every draw some clip has all 8.
All inputs are finite; a program needn't handle non-finite values.
Results may differ from the reference program's by a relative error of at most 0.0051.
Values may be sent and summed in bfloat16 or wider, within the bound.
No kernel may reach another device: no remote copies, remote signals or barrier semaphores. Data moves between devices by JAX's collectives and lax.ppermute only.
A program may use at most 64 MiB of HBM per device.

```python
import jax
import jax.numpy as jnp
from jax import lax

CH = 384
GROUPS = 32
CLIPS = 2
COLS = 64
FRAMES = 8
ROWS = 4


def draw_frame_counts(key, part):
    first_key, second_key = jax.random.split(jax.random.fold_in(key, 11))
    others = jax.random.randint(first_key, (CLIPS,), 1, FRAMES)
    full_at = jax.random.randint(second_key, (), 0, CLIPS)
    clip_ids = jnp.arange(CLIPS)
    return jnp.where(clip_ids == full_at, FRAMES, others).astype(jnp.int32)


def shard_levels(rng, dims, shards, low, top_value):
    gain = 1.0
    for position, shards_of in shards:
        heights = jax.random.uniform(jax.random.fold_in(jax.random.fold_in(rng, 6), position), (shards_of,), jnp.float32, low / len(shards), top_value / len(shards))
        gain = gain * jnp.repeat(jnp.exp(heights), dims[position] // shards_of).reshape((-1,) + (1,) * (len(dims) - 1 - position))
    return gain


def normal_values(own_key, dims, spread, reach, shards=(), kind=jnp.bfloat16):
    gain = shard_levels(own_key, dims, shards, -0.22, 0.18) if shards else 1.0
    result = jax.random.normal(own_key, dims, jnp.float32) * spread * gain
    return jnp.minimum(jnp.maximum(result, -reach), reach).astype(kind)


def setup_inputs(seed: int = 0, part: int = 0) -> dict:
    key_of = jax.random.split(jax.random.key(seed), 9)
    own_keys = jax.random.split(jax.random.fold_in(key_of[8], part), 9)
    return {
        "latents": normal_values(own_keys[0], (CLIPS, FRAMES, ROWS, COLS, CH), 1.0, 6.0, ((1, 4), (2, 2))),
        "frame_counts": draw_frame_counts(jax.random.fold_in(jax.random.fold_in(key_of[8], part), 71), part),
        "norm_gain": jnp.clip(1.0 + 0.18 * jax.random.normal(key_of[2], (CH,), jnp.float32), 0.1, 1.9),
        "norm_bias": normal_values(key_of[3], (CH,), 0.5, 3.0, (), jnp.float32),
        "conv3_weight": normal_values(key_of[4], (3, 3, 3, CH, CH), (27 * CH) ** -0.5, 0.0625),
        "conv3_bias": normal_values(key_of[5], (CH,), 0.5, 3.0, (), jnp.float32),
        "conv2_weight": normal_values(key_of[6], (3, 3, CH, CH), (9 * CH) ** -0.5, 0.109375),
        "conv2_bias": normal_values(key_of[7], (CH,), 0.5, 3.0, (), jnp.float32),
    }


epsilon = 1e-05

def reference(latents, frame_counts, norm_gain, norm_bias, conv3_weight, conv3_bias, conv2_weight, conv2_bias):
    clips, frames, rows, columns, channels = latents.shape
    per_group = channels // GROUPS
    frame_ids = jnp.arange(frames, dtype=jnp.int32)
    frame_mask = (frame_ids[None, :] < frame_counts[:, None]).astype(jnp.float32)
    broad_mask = frame_mask[:, :, None, None, None]
    values = latents.astype(jnp.float32)
    grouped = (values * broad_mask).reshape(clips, frames, rows, columns, GROUPS, per_group)
    first = lax.optimization_barrier(jnp.sum(grouped, axis=(1, 2, 3, 5)))
    second = lax.optimization_barrier(jnp.sum(grouped * grouped, axis=(1, 2, 3, 5)))
    cells = (frame_counts * (rows * columns * per_group)).astype(jnp.float32)[:, None]
    mean = first / cells
    variance = second / cells - mean * mean
    scale = lax.rsqrt(variance + epsilon)
    mean_ch = jnp.repeat(mean, per_group, axis=1)[:, None, None, None, :]
    scale_ch = jnp.repeat(scale, per_group, axis=1)[:, None, None, None, :]
    activated = (jax.nn.silu((values - mean_ch) * scale_ch * norm_gain + norm_bias) * broad_mask).astype(jnp.bfloat16)
    convolved = lax.conv_general_dilated(activated.astype(jnp.float32), conv3_weight.astype(jnp.float32), (1, 1, 1), ((2, 0), (1, 1), (1, 1)), dimension_numbers=('NDHWC', 'DHWIO', 'NDHWC'), precision=lax.Precision.HIGHEST)
    middle = ((values + convolved + conv3_bias) * broad_mask).astype(jnp.bfloat16)
    upsampled = jnp.repeat(jnp.repeat(middle, 2, axis=2), 2, axis=3)
    flat = upsampled.reshape(clips * frames, 2 * rows, 2 * columns, channels).astype(jnp.float32)
    planar = lax.conv_general_dilated(flat, conv2_weight.astype(jnp.float32), (1, 1), ((1, 1), (1, 1)), dimension_numbers=('NHWC', 'HWIO', 'NHWC'), precision=lax.Precision.HIGHEST)
    planar = planar.reshape(clips, frames, 2 * rows, 2 * columns, channels)
    return ((planar + conv2_bias) * broad_mask).astype(jnp.bfloat16)
```

```python
import functools

import jax
import jax.numpy as jnp
from jax import lax
from jax.experimental import pallas as pl
from jax.experimental.pallas import tpu as pltpu
from jax.sharding import PartitionSpec as P

GROUPS = 32
EPSILON = 1e-05
MIB = 1 << 20

VMEM = pl.BlockSpec(memory_space=pltpu.VMEM)
SMEM = pl.BlockSpec(memory_space=pltpu.SMEM)
ANY = pl.BlockSpec(memory_space=pl.ANY)


def edge_rows(rows, count, place):
    if count == 2:
        return [jnp.where(place == 0, rows - 1, 0)]
    return [0, rows - 1]


def exchange(edges, axis):
    count = lax.axis_size(axis)
    if count == 2:
        other = lax.ppermute(edges[0], axis, [(0, 1), (1, 0)])
        return other, other
    first, last = edges
    above = lax.ppermute(last, axis, [(i, (i + 1) % count) for i in range(count)])
    below = lax.ppermute(first, axis, [((i + 1) % count, i) for i in range(count)])
    return above, below


def all_sum(value, axis):
    count = lax.axis_size(axis)
    if count & (count - 1):
        return lax.psum(value, axis)
    step = 1
    while step < count:
        value = value + lax.ppermute(value, axis, [(i, i ^ step) for i in range(count)])
        step *= 2
    return value


def stats_kernel(frames, count, scal, x, sums, *edges):
    clips, _, rows, columns, channels = x.shape
    parts = []
    for c in range(clips):
        first = jnp.zeros((columns, channels), jnp.float32)
        second = jnp.zeros((columns, channels), jnp.float32)
        for f in range(frames):
            keep = scal[0] + f < scal[2 + c]
            for r in range(rows):
                v = jnp.where(keep, x[c, f, r].astype(jnp.float32), 0.0)
                first = first + v
                second = second + v * v
        parts.append(jnp.sum(first, axis=0, keepdims=True))
        parts.append(jnp.sum(second, axis=0, keepdims=True))
    total = jnp.concatenate(parts, axis=0)
    high = total.astype(jnp.bfloat16)
    rest = total - high.astype(jnp.float32)
    middle = rest.astype(jnp.bfloat16)
    low = (rest - middle.astype(jnp.float32)).astype(jnp.bfloat16)
    width = channels // GROUPS
    group = lambda dim: jnp.floor(
        (lax.broadcasted_iota(jnp.int32, (channels, channels), dim).astype(jnp.float32) + 0.5)
        * (1.0 / width)
    )
    same = (group(0) == group(1)).astype(jnp.bfloat16)
    split = jnp.concatenate([high, middle, low], axis=0)
    summed = jnp.dot(split, same, preferred_element_type=jnp.float32)
    n = 2 * clips
    sums[...] = summed[:n] + summed[n : 2 * n] + summed[2 * n :]
    for e, row in zip(edges, edge_rows(rows, count, scal[1])):
        e[...] = x[:, :, pl.ds(row, 1)]


def shifted(value, step):
    size = value.shape[0]
    at = lax.broadcasted_iota(jnp.int32, value.shape, 0)
    rolled = pltpu.roll(value, step % size, 0)
    return jnp.where(at == (0 if step > 0 else size - 1), 0.0, rolled)


def put_three(dst, index, value, channels):
    dst[(*index, slice(None), slice(channels, 2 * channels))] = value.astype(jnp.bfloat16)
    dst[(*index, slice(None), slice(0, channels))] = shifted(value, 1).astype(jnp.bfloat16)
    dst[(*index, slice(None), slice(2 * channels, 3 * channels))] = shifted(value, -1).astype(jnp.bfloat16)


def block_kernel(
    count, per_count, scal, sums, gain, bias, bias3, own, own_top, own_bottom, past, past_top, past_bottom,
    weight, mid, *rest
):
    edges, (act, kern, sem) = rest[:-3], rest[-3:]
    clips, frames, rows, columns, channels = own.shape
    taps = weight.shape[0]
    span = 3 * channels
    copies = []
    for a in range(taps):
        copies.append(
            pltpu.make_async_copy(
                weight.at[taps - 1 - a], kern.at[:, pl.ds(a * channels, channels)], sem.at[a]
            )
        )
        copies[-1].start()
    place = scal[1]
    for c in range(clips):
        n = (scal[2 + c] * per_count).astype(jnp.float32)
        mean = sums[2 * c : 2 * c + 1, :] / n
        variance = sums[2 * c + 1 : 2 * c + 2, :] / n - mean * mean
        scale = lax.rsqrt(variance + EPSILON) * gain[...]
        offset = bias[...] - mean * scale
        for f in range(2 + frames):
            if f < 2:
                body, top, bottom, at = past, past_top, past_bottom, f + frames - 2
            else:
                body, top, bottom, at = own, own_top, own_bottom, f - 2
            moment = scal[0] + f - 2
            live = jnp.logical_and(moment >= 0, moment < scal[2 + c])
            for r in range(rows + 2):
                if r == 0:
                    raw, keep = top[c, at, 0], jnp.logical_and(live, place > 0)
                elif r == rows + 1:
                    raw, keep = bottom[c, at, 0], jnp.logical_and(live, place < count - 1)
                else:
                    raw, keep = body[c, at, r - 1], live
                v = raw.astype(jnp.float32) * scale + offset
                v = v / (1.0 + jnp.exp(-v))
                put_three(act, (f, r, c), jnp.where(keep, v, 0.0), channels)
    size = rows * clips * columns

    def left(f):
        return jnp.concatenate(
            [act[f, b : b + rows].reshape(size, span) for b in range(3)], axis=1
        )

    def part(f, low, high):
        return jnp.dot(
            left(f), kern[:, low * channels : high * channels], preferred_element_type=jnp.float32
        )

    for copy in copies:
        copy.wait()
    assert frames == 2 and taps == 3
    two = part(2, 0, 2)
    out = [two[:, :channels], two[:, channels:] + part(3, 0, 1)]
    one = part(1, 1, 3)
    out = [out[0] + one[:, :channels] + part(0, 2, 3), out[1] + one[:, channels:]]
    for f in range(frames):
        for c in range(clips):
            live = scal[0] + f < scal[2 + c]
            for r in range(rows):
                start = (r * clips + c) * columns
                value = own[c, f, r].astype(jnp.float32) + out[f][start : start + columns] + bias3[...]
                mid[r, f, c] = jnp.where(live, value, 0.0).astype(jnp.bfloat16)
    for e, row in zip(edges, edge_rows(rows, count, place)):
        e[...] = mid[pl.ds(row, 1)]


def fold_kernel(weight, out):
    taps = ((((0,), (1, 2)), ((0, 1), (2,))))
    for p in range(2):
        for r in range(2):
            by_column = []
            for e in range(3):
                total = None
                for b in taps[p][r]:
                    v = weight[b, e].astype(jnp.float32)
                    total = v if total is None else total + v
                by_column.append(total)
            for q in range(2):
                for s in range(2):
                    total = None
                    for e in taps[q][s]:
                        total = by_column[e] if total is None else total + by_column[e]
                    out[p, q, r, s] = total.astype(jnp.bfloat16)


def planar_kernel(count, scal, mid, top, bottom, kern, bias2, out, wide, lines):
    rows, frames, clips, columns, channels = mid.shape
    place = scal[1]
    for r in range(rows + 2):
        for f in range(frames):
            for c in range(clips):
                if r == 0:
                    v = jnp.where(place > 0, top[0, f, c].astype(jnp.float32), 0.0)
                elif r == rows + 1:
                    v = jnp.where(place < count - 1, bottom[0, f, c].astype(jnp.float32), 0.0)
                else:
                    v = mid[r - 1, f, c].astype(jnp.float32)
                put_three(wide, (r, f, c), v, channels)
    size = rows * frames * clips * columns
    for p in range(2):
        for q in range(2):
            low = q * channels
            left = jnp.concatenate(
                [
                    wide[p + r : p + r + rows, :, :, :, low : low + 2 * channels].reshape(size, 2 * channels)
                    for r in range(2)
                ],
                axis=1,
            )
            part = jnp.dot(
                left, kern[p, q].reshape(4 * channels, channels), preferred_element_type=jnp.float32
            )
            for i in range(rows):
                for f in range(frames):
                    for c in range(clips):
                        start = ((i * frames + f) * clips + c) * columns
                        for k in range(channels // 128):
                            lines[k, (i * frames + f) * clips + c, pl.ds(q, columns, stride=2), :] = part[
                                start : start + columns, k * 128 : k * 128 + 128
                            ]
        for i in range(rows):
            for f in range(frames):
                for c in range(clips):
                    live = scal[0] + f < scal[2 + c]
                    for k in range(channels // 128):
                        lanes = slice(k * 128, k * 128 + 128)
                        value = lines[k, (i * frames + f) * clips + c] + bias2[:, lanes]
                        out[c, f, 2 * i + p, :, lanes] = jnp.where(live, value, 0.0).astype(jnp.bfloat16)


def body(
    latents, frame_counts, norm_gain, norm_bias, conv3_weight, conv3_bias, conv2_weight, conv2_bias
):
    clips, frames, rows, columns, channels = latents.shape
    count = lax.axis_size("space")
    behind = lax.axis_size("tm")
    per_count = rows * count * columns * (channels // GROUPS)
    scal = jnp.concatenate(
        [
            jnp.stack([lax.axis_index("tm") * frames, lax.axis_index("space")]).astype(jnp.int32),
            frame_counts,
        ]
    )
    params = lambda mib: pltpu.CompilerParams(vmem_limit_bytes=mib * MIB)
    n_edges = 1 if count == 2 else 2
    f32, bf16 = jnp.float32, jnp.bfloat16
    shape = jax.ShapeDtypeStruct
    cost = lambda flops, size: pl.CostEstimate(flops=int(flops), bytes_accessed=int(size), transcendentals=0)

    past = lax.ppermute(latents, "tm", [(i, (i + 1) % behind) for i in range(behind)])
    stats = pl.pallas_call(
        functools.partial(stats_kernel, frames, count),
        out_shape=[shape((2 * clips, channels), f32)]
        + [shape((clips, frames, 1, columns, channels), bf16)] * n_edges,
        in_specs=[SMEM, VMEM],
        out_specs=[VMEM] * (1 + n_edges),
        compiler_params=params(8),
        name="stats",
    )(scal, latents)
    sums = all_sum(all_sum(stats[0], "space"), "tm")
    own_top, own_bottom = exchange(stats[1:], "space")
    place = lax.axis_index("space")
    past_edges = [
        lax.dynamic_slice_in_dim(past, row, 1, axis=2) for row in edge_rows(rows, count, place)
    ]
    past_top, past_bottom = exchange(past_edges, "space")

    folded = pl.pallas_call(
        fold_kernel,
        out_shape=shape((2, 2, 2, 2, channels, channels), bf16),
        in_specs=[VMEM],
        out_specs=VMEM,
        compiler_params=params(16),
        cost_estimate=cost(4e7, 8e6),
        name="fold",
    )(conv2_weight)

    taps = conv3_weight.shape[0]
    line = lambda v: v.reshape(1, channels)
    block = pl.pallas_call(
        functools.partial(block_kernel, count, per_count),
        out_shape=[shape((rows, frames, clips, columns, channels), bf16)]
        + [shape((1, frames, clips, columns, channels), bf16)] * n_edges,
        in_specs=[SMEM] + [VMEM] * 10 + [ANY],
        out_specs=[VMEM] * (1 + n_edges),
        scratch_shapes=[
            pltpu.VMEM((frames + 2, rows + 2, clips, columns, 3 * channels), bf16),
            pltpu.VMEM((9 * channels, taps * channels), bf16),
            pltpu.SemaphoreType.DMA((taps,)),
        ],
        compiler_params=params(40),
        cost_estimate=cost(4e9, 1e7),
        name="block",
    )(
        scal, sums, line(norm_gain), line(norm_bias), line(conv3_bias), latents, own_top, own_bottom,
        past, past_top, past_bottom, conv3_weight.reshape(taps, 9 * channels, channels),
    )
    mid = block[0]
    mid_top, mid_bottom = exchange(block[1:], "space")
    return pl.pallas_call(
        functools.partial(planar_kernel, count),
        out_shape=shape((clips, frames, 2 * rows, 2 * columns, channels), bf16),
        in_specs=[SMEM] + [VMEM] * 5,
        out_specs=VMEM,
        scratch_shapes=[
            pltpu.VMEM((rows + 2, frames, clips, columns, 3 * channels), bf16),
            pltpu.VMEM((channels // 128, rows * frames * clips, 2 * columns, 128), f32),
        ],
        compiler_params=params(40),
        cost_estimate=cost(3e9, 8e6),
        name="planar",
    )(scal, mid, mid_top, mid_bottom, folded, line(conv2_bias))


def solution(mesh):
    placed = (P("clip", "tm", "space", None, None), P("clip"), P(), P(), P(), P(), P(), P())
    return jax.shard_map(
        body,
        mesh=mesh,
        in_specs=placed,
        out_specs=P("clip", "tm", "space", None, None),
        check_vma=False,
    )
```

```python
import functools

import jax
import jax.numpy as jnp
from jax import lax
from jax.experimental import pallas as pl
from jax.experimental.pallas import tpu as pltpu
from jax.sharding import PartitionSpec as P

GROUPS = 32
EPSILON = 1e-05
MIB = 1 << 20
LANES = 128

VMEM = pl.BlockSpec(memory_space=pltpu.VMEM)
SMEM = pl.BlockSpec(memory_space=pltpu.SMEM)
HBM = pl.BlockSpec(memory_space=pltpu.HBM)
f32, bf16 = jnp.float32, jnp.bfloat16


def edge_rows(rows, count):
    if count == 2:
        return [jnp.where(lax.axis_index("space") == 0, rows - 1, 0)]
    return [0, rows - 1]


def exchange(edges, axis):
    count = lax.axis_size(axis)
    if count == 2:
        other = lax.ppermute(edges[0], axis, [(0, 1), (1, 0)])
        return other, other
    first, last = edges
    above = lax.ppermute(last, axis, [(i, (i + 1) % count) for i in range(count)])
    below = lax.ppermute(first, axis, [((i + 1) % count, i) for i in range(count)])
    return above, below


def all_sum(value, axis):
    count = lax.axis_size(axis)
    if count & (count - 1):
        return lax.psum(value, axis)
    step = 1
    while step < count:
        value = value + lax.ppermute(value, axis, [(i, i ^ step) for i in range(count)])
        step *= 2
    return value


def shifted(value, step):
    size = value.shape[0]
    at = lax.broadcasted_iota(jnp.int32, value.shape, 0)
    rolled = pltpu.roll(value, step % size, 0)
    return jnp.where(at == (0 if step > 0 else size - 1), 0.0, rolled)


def stats_kernel(count, counts, x, sums, *rest):
    clips, frames, rows, columns, channels = x.shape
    own, edges, sem = rest[:clips], rest[clips:-1], rest[-1]
    copies = []
    for c in range(clips):
        copies.append([])
        for f in range(frames):
            copies[c].append(pltpu.make_async_copy(x.at[c, f], own[c].at[f], sem.at[c, f]))
            copies[c][f].start()
    width = channels // GROUPS
    group = lambda dim: jnp.floor(
        (lax.broadcasted_iota(jnp.int32, (channels, channels), dim).astype(f32) + 0.5) * (1.0 / width)
    )
    same = (group(0) == group(1)).astype(bf16)
    start = lax.axis_index("tm") * frames
    parts = []
    for c in range(clips):
        first = jnp.zeros((columns, channels), f32)
        second = jnp.zeros((columns, channels), f32)
        for f in range(frames):
            copies[c][f].wait()
            keep = start + f < counts[c]
            for r in range(rows):
                v = jnp.where(keep, own[c][f, r].astype(f32), 0.0)
                first = first + v
                second = second + v * v
        parts.append(jnp.sum(first, axis=0, keepdims=True))
        parts.append(jnp.sum(second, axis=0, keepdims=True))
    total = jnp.concatenate(parts, axis=0)
    high = total.astype(bf16)
    left = total - high.astype(f32)
    middle = left.astype(bf16)
    low = (left - middle.astype(f32)).astype(bf16)
    split = jnp.concatenate([high, middle, low], axis=0)
    summed = jnp.dot(split, same, preferred_element_type=f32)
    n = 2 * clips
    sums[...] = summed[:n] + summed[n : 2 * n] + summed[2 * n :]
    for e, row in zip(edges, edge_rows(rows, count)):
        for c in range(clips):
            e[c] = own[c][:, pl.ds(row, 1)]


def activate(act, index, raw, keep, scale, offset):
    v = raw.astype(f32) * scale + offset
    v = v / (1.0 + jnp.exp(-v))
    act[index] = jnp.where(keep, v, 0.0).astype(bf16)


def keep_row(r, rows, count, live):
    place = lax.axis_index("space")
    if r == 0:
        return jnp.logical_and(live, place > 0)
    if r == rows + 1:
        return jnp.logical_and(live, place < count - 1)
    return live


def patch(act, f, rows):
    channels = act.shape[-1]
    return jnp.concatenate(
        [act[f, b : b + rows].reshape(-1, channels) for b in range(3)], axis=1
    )


def own_kernel(
    count, per_count, counts, sums, gain, bias, *rest
):
    clips = counts.shape[0]
    own, (top, bottom, weight), (acc, norm, past_kern, act, kern, sem) = rest[:clips], rest[clips : clips + 3], rest[clips + 3 :]
    frames, rows, columns, channels = own[0].shape
    copies = {}
    for a in (2, 1, 0):
        dst = kern if a == 2 else past_kern.at[pl.ds(3 * a, 3)]
        for e in range(3):
            copy = pltpu.make_async_copy(
                weight.at[a, :, e], dst.at[:, :, pl.ds(e * channels, channels)], sem.at[a, e]
            )
            copy.start()
            copies.setdefault(a, []).append(copy)
    start = lax.axis_index("tm") * frames
    for c in range(clips):
        n = (counts[c] * per_count).astype(f32)
        mean = sums[2 * c : 2 * c + 1, :] / n
        variance = sums[2 * c + 1 : 2 * c + 2, :] / n - mean * mean
        scale = lax.rsqrt(variance + EPSILON) * gain[...].reshape(1, channels)
        offset = bias[...].reshape(1, channels) - mean * scale
        norm[c, 0:1] = scale
        norm[c, 1:2] = offset
    for f in range(frames):
        for c in range(clips):
            scale, offset = norm[c, 0:1], norm[c, 1:2]
            live = start + f < counts[c]
            for r in range(rows + 2):
                raw = top[c, f, 0] if r == 0 else bottom[c, f, 0] if r == rows + 1 else own[c][f, r - 1]
                activate(act, (f, r, c), raw, keep_row(r, rows, count, live), scale, offset)
    span = 3 * channels

    def store(t, part):
        for r in range(rows):
            for c in range(clips):
                low = (r * clips + c) * columns
                block = part[low : low + columns]
                acc[t, c, r] = (
                    shifted(block[:, :channels], 1)
                    + block[:, channels : 2 * channels]
                    + shifted(block[:, 2 * channels :], -1)
                )

    assert frames == 2
    for copy in copies[2]:
        copy.wait()
    store(0, jnp.dot(patch(act, 0, rows), kern[...].reshape(span, span), preferred_element_type=f32))
    for copy in copies[1]:
        copy.wait()
    both = jnp.concatenate([past_kern[3:6].reshape(span, span), kern[...].reshape(span, span)], axis=0)
    store(
        1,
        jnp.dot(
            jnp.concatenate([patch(act, 0, rows), patch(act, 1, rows)], axis=1),
            both,
            preferred_element_type=f32,
        ),
    )
    for copy in copies[0]:
        copy.wait()


def past_kernel(
    count, clip, counts, norm, bias3, acc, past_kern, own, past, top, bottom, mid, *rest
):
    edges, act = rest[:-1], rest[-1]
    frames, rows, columns, channels = own.shape
    span = 3 * channels
    start = lax.axis_index("tm") * frames
    scale, offset = norm[clip, 0:1], norm[clip, 1:2]
    for g in range(2):
        at = frames - 2 + g
        moment = start - 2 + g
        live = jnp.logical_and(moment >= 0, moment < counts[clip])
        for r in range(rows + 2):
            raw = top[at, 0] if r == 0 else bottom[at, 0] if r == rows + 1 else past[at, r - 1]
            activate(act, (g, r), raw, keep_row(r, rows, count, live), scale, offset)

    def store(t, part):
        live = start + t < counts[clip]
        for r in range(rows):
            block = part[r * columns : (r + 1) * columns]
            value = (
                shifted(block[:, :channels], 1)
                + block[:, channels : 2 * channels]
                + shifted(block[:, 2 * channels :], -1)
            )
            value = value + acc[t, clip, r] + own[t, r].astype(f32) + bias3[...].reshape(1, channels)
            mid[r, t] = jnp.where(live, value, 0.0).astype(bf16)

    older, newer = patch(act, 0, rows), patch(act, 1, rows)
    store(1, jnp.dot(newer, past_kern[0:3].reshape(span, span), preferred_element_type=f32))
    store(
        0,
        jnp.dot(
            jnp.concatenate([older, newer], axis=1),
            past_kern[...].reshape(2 * span, span),
            preferred_element_type=f32,
        ),
    )
    for e, row in zip(edges, edge_rows(rows, count)):
        e[...] = mid[pl.ds(row, 1)]


PHASES = (((0,), (1, 2)), ((0, 1), (2,)))


def fold_kernel(weight, out):
    channels = weight.shape[-1]
    for p in range(2):
        for r in range(2):
            by_column = []
            for e in range(3):
                total = None
                for b in PHASES[p][r]:
                    v = weight[b, e].astype(f32)
                    total = v if total is None else total + v
                by_column.append(total)
            for q in range(2):
                for s in range(2):
                    total = None
                    for e in PHASES[q][s]:
                        total = by_column[e] if total is None else total + by_column[e]
                    low = (2 * q + s) * channels
                    out[p, r, :, low : low + channels] = total.astype(bf16)


def planar_kernel(count, clip, counts, mid, top, bottom, kern, bias2, *rest):
    out, wide, lines, ready, sem = rest[-5:]
    rows, frames, columns, channels = mid.shape
    start = lax.axis_index("tm") * frames
    for r in range(rows + 2):
        if 0 < r <= rows:
            wide[r] = mid[r - 1]
        else:
            side = top if r == 0 else bottom
            keep = keep_row(r, rows, count, start >= 0)
            wide[r] = jnp.where(keep, side[0].astype(f32), 0.0).astype(bf16)
    copies = []
    for p in range(2):
        left = jnp.concatenate(
            [wide[p + r : p + r + rows].reshape(-1, channels) for r in range(2)], axis=1
        )
        part = jnp.dot(left, kern[p].reshape(2 * channels, 4 * channels), preferred_element_type=f32)
        for i in range(rows):
            for f in range(frames):
                n = i * frames + f
                block = part[n * columns : (n + 1) * columns]
                cut = lambda m: block[:, m * channels : (m + 1) * channels]
                even = cut(1) + shifted(cut(0), 1)
                odd = cut(2) + shifted(cut(3), -1)
                live = start + f < counts[clip]
                for k in range(channels // LANES):
                    lanes = slice(k * LANES, (k + 1) * LANES)
                    lines[k, n, pl.ds(0, columns, stride=2), :] = even[:, lanes]
                    lines[k, n, pl.ds(1, columns, stride=2), :] = odd[:, lanes]
                    value = lines[k, n] + bias2[...].reshape(1, channels)[:, lanes]
                    ready[f, 2 * i + p, :, lanes] = jnp.where(live, value, 0.0).astype(bf16)
                copies.append(
                    pltpu.make_async_copy(
                        ready.at[f, 2 * i + p], out.at[clip, f, 2 * i + p], sem.at[f, 2 * i + p]
                    )
                )
                copies[-1].start()
    for copy in copies:
        copy.wait()


def body(
    latents, frame_counts, norm_gain, norm_bias, conv3_weight, conv3_bias, conv2_weight, conv2_bias
):
    clips, frames, rows, columns, channels = latents.shape
    count = lax.axis_size("space")
    behind = lax.axis_size("tm")
    per_count = rows * count * columns * (channels // GROUPS)
    params = lambda mib: pltpu.CompilerParams(vmem_limit_bytes=mib * MIB)
    n_edges = 1 if count == 2 else 2
    shape = jax.ShapeDtypeStruct
    cost = lambda flops, size: pl.CostEstimate(flops=int(flops), bytes_accessed=int(size), transcendentals=0)
    span = 3 * channels

    stats = pl.pallas_call(
        functools.partial(stats_kernel, count),
        out_shape=[shape((2 * clips, channels), f32)]
        + [shape((frames, rows, columns, channels), bf16)] * clips
        + [shape((clips, frames, 1, columns, channels), bf16)] * n_edges,
        in_specs=[SMEM, HBM],
        out_specs=[VMEM] * (1 + clips + n_edges),
        scratch_shapes=[pltpu.SemaphoreType.DMA((clips, frames))],
        compiler_params=params(8),
        cost_estimate=cost(1e6, 8e5),
        name="stats",
    )(frame_counts, latents)
    own, own_edges = stats[1 : 1 + clips], stats[1 + clips :]
    sums = all_sum(all_sum(stats[0], "space"), "tm")
    own_top, own_bottom = exchange(own_edges, "space")
    past = [lax.ppermute(x, "tm", [(i, i + 1) for i in range(behind - 1)]) for x in own]
    past_sides = [
        exchange([lax.dynamic_slice_in_dim(x, row, 1, axis=1) for row in edge_rows(rows, count)], "space")
        for x in past
    ]

    folded = pl.pallas_call(
        fold_kernel,
        out_shape=shape((2, 2, channels, 4 * channels), bf16),
        in_specs=[VMEM],
        out_specs=VMEM,
        compiler_params=params(16),
        cost_estimate=cost(4e7, 8e6),
        name="fold",
    )(conv2_weight)

    acc, norm, past_kern = pl.pallas_call(
        functools.partial(own_kernel, count, per_count),
        out_shape=[
            shape((frames, clips, rows, columns, channels), f32),
            shape((clips, 2, channels), f32),
            shape((6, channels, span), bf16),
        ],
        in_specs=[SMEM] + [VMEM] * (5 + clips) + [HBM],
        out_specs=[VMEM] * 3,
        scratch_shapes=[
            pltpu.VMEM((frames, rows + 2, clips, columns, channels), bf16),
            pltpu.VMEM((3, channels, span), bf16),
            pltpu.SemaphoreType.DMA((3, 3)),
        ],
        compiler_params=params(24),
        cost_estimate=cost(2e9, 1e7),
        name="own",
    )(frame_counts, sums, norm_gain, norm_bias, *own, own_top, own_bottom, conv3_weight)

    out = None
    blocks = []
    for c in range(clips):
        blocks.append(
            pl.pallas_call(
                functools.partial(past_kernel, count, c),
                out_shape=[shape((rows, frames, columns, channels), bf16)]
                + [shape((1, frames, columns, channels), bf16)] * n_edges,
                in_specs=[SMEM] + [VMEM] * 8,
                out_specs=[VMEM] * (1 + n_edges),
                scratch_shapes=[pltpu.VMEM((2, rows + 2, columns, channels), bf16)],
                compiler_params=params(16),
                cost_estimate=cost(1e9, 6e6),
                name=f"past{c}",
            )(frame_counts, norm, conv3_bias, acc, past_kern, own[c], past[c], *past_sides[c])
        )
    for c in range(clips):
        mid = blocks[c][0]
        top, bottom = exchange(blocks[c][1:], "space")
        out = pl.pallas_call(
            functools.partial(planar_kernel, count, c),
            out_shape=shape((clips, frames, 2 * rows, 2 * columns, channels), bf16),
            in_specs=[SMEM] + [VMEM] * 5 + ([HBM] if c else []),
            out_specs=HBM,
            scratch_shapes=[
                pltpu.VMEM((rows + 2, frames, columns, channels), bf16),
                pltpu.VMEM((channels // LANES, rows * frames, 2 * columns, LANES), f32),
                pltpu.VMEM((frames, 2 * rows, 2 * columns, channels), bf16),
                pltpu.SemaphoreType.DMA((frames, 2 * rows)),
            ],
            input_output_aliases={6: 0} if c else {},
            compiler_params=params(16),
            cost_estimate=cost(1.3e9, 6e6),
            name=f"planar{c}",
        )(frame_counts, mid, top, bottom, folded, conv2_bias, *([out] if c else []))
    return out


def solution(mesh):
    placed = (P("clip", "tm", "space", None, None), P("clip"), P(), P(), P(), P(), P(), P())
    return jax.shard_map(
        body,
        mesh=mesh,
        in_specs=placed,
        out_specs=P("clip", "tm", "space", None, None),
        check_vma=False,
    )
```
